128 devices in a mesh: seq: 32 (over z_hi, y, x), ch: 4 (over z_lo, core).
Axes of the slice: x: 4, y: 4, z: 4 (z_hi: 2, z_lo: 2; z = z_hi * 2 + z_lo), core: 2. Of those that a mesh axis runs over, the one named last changes fastest.
Arguments:
- tokens: bfloat16 [262144, 512], P('seq', 'ch'), may hold values from -6 to 6
- gate: bfloat16 [262144, 512], P('seq', 'ch'), may hold values from -6 to 6
- cotangent: bfloat16 [262144, 512], P('seq', 'ch'), may hold values from -6 to 6
- w_first: bfloat16 [1024, 1024], replicated, may hold values from -0.1875 to 0.1875
- w_second: bfloat16 [256, 256], replicated, may hold values from -0.375 to 0.375
Outputs:
- mixed: bfloat16 [262144, 512], P('seq', 'ch')
- grad_tokens: bfloat16 [262144, 512], P('seq', 'ch')
- grad_gate: bfloat16 [262144, 512], P('seq', 'ch')
- grad_first: float32 [1024, 1024], replicated
- grad_second: float32 [256, 256], replicated
The draws below stay inside these ranges and needn't reach their ends.
All inputs are finite; a program needn't handle non-finite values.
Results may differ from the reference program's by a relative error of at most 0.0058.
Values may be sent and summed in bfloat16 or wider, within the bound.
No kernel may reach another device: no remote copies, remote signals or barrier semaphores. Data moves between devices by JAX's collectives and lax.ppermute only.
A program may use at most 128 MiB of HBM per device.

```python
import jax
import jax.numpy as jnp

BLK = 1024
C = 512
NB = 256
TOKENS = 262144


def block_levels(stream_key, shape, cuts, smallest, top_value):
    factor_of, own = 1.0, jax.random.fold_in(stream_key, 6)
    for position, parts in cuts:
        steps = jnp.exp(jax.random.uniform(jax.random.fold_in(own, position), (parts,), jnp.float32, smallest / len(cuts), top_value / len(cuts)))
        factor_of = factor_of * jnp.repeat(steps, shape[position] // parts).reshape([-1 if axis == position else 1 for axis in range(len(shape))])
    return factor_of


def normal_values(rng, extent, width, bound, split=(), dtype=jnp.bfloat16):
    drawn = width * jax.random.normal(rng, extent, jnp.float32)
    if split:
        drawn = drawn * block_levels(rng, extent, split, -0.22, 0.18)
    return jnp.clip(drawn, -bound, bound).astype(dtype)


def setup_inputs(seed: int = 0) -> dict:
    key_of = jax.random.split(jax.random.key(seed), 6)
    return {
        "tokens": normal_values(key_of[0], (TOKENS, C), 1.0, 6.0, ((0, 32), (1, 4))),
        "gate": normal_values(key_of[1], (TOKENS, C), 1.5, 6.0, ((0, 32), (1, 4))),
        "cotangent": normal_values(key_of[2], (TOKENS, C), 1.0, 6.0, ((0, 32), (1, 4))),
        "w_first": normal_values(key_of[3], (BLK, BLK), BLK ** -0.5, 0.1875),
        "w_second": normal_values(key_of[4], (NB, NB), NB ** -0.5, 0.375),
    }


def reference(tokens, gate, cotangent, w_first, w_second):
    x = tokens.reshape(NB, BLK, C)
    g = gate.reshape(NB, BLK, C).astype(jnp.float32)
    dz = cotangent.reshape(NB, BLK, C).astype(jnp.float32)
    w1 = w_first.astype(jnp.float32)
    w2 = w_second.astype(jnp.float32)
    first = jnp.einsum('jk,ikc->ijc', w1, x.astype(jnp.float32))
    sig = jax.nn.sigmoid(g)
    act = g * sig
    slope = sig * (1.0 + g * (1.0 - sig))
    hidden = (first * act).astype(jnp.bfloat16)
    hidden32 = hidden.astype(jnp.float32)
    mixed = jnp.einsum('il,ljc->ijc', w2, hidden32).astype(jnp.bfloat16)
    grad_hidden = jnp.einsum('il,ijc->ljc', w2, dz).astype(jnp.bfloat16)
    grad_second = jnp.einsum('ijc,ljc->il', dz, hidden32) / jnp.sqrt(jnp.float32(BLK * C))
    gh32 = grad_hidden.astype(jnp.float32)
    grad_first_act = (gh32 * act).astype(jnp.bfloat16)
    grad_gate = (gh32 * first * slope).astype(jnp.bfloat16)
    gfa32 = grad_first_act.astype(jnp.float32)
    grad_tokens = jnp.einsum('jk,ijc->ikc', w1, gfa32).astype(jnp.bfloat16)
    grad_first = jnp.einsum('ijc,ikc->jk', gfa32, x.astype(jnp.float32)) / jnp.sqrt(jnp.float32(NB * C))
    return (mixed.reshape(TOKENS, C), grad_tokens.reshape(TOKENS, C), grad_gate.reshape(TOKENS, C), grad_first, grad_second)
```

```python
import jax
import jax.numpy as jnp
from jax import lax
from jax.experimental import pallas as pl
from jax.experimental.pallas import tpu as pltpu
from jax.sharding import PartitionSpec as P

BF = jnp.bfloat16
F32 = jnp.float32
LANES = 128


def gates(g):
    sig = jax.nn.sigmoid(g)
    return g * sig, sig * (1.0 + g * (1.0 - sig))


def front(x, g, w_first, tj):
    lb, block, width = x.shape

    def body(x_ref, g_ref, w_ref, hid_ref, first_ref, wide, turn):
        @pl.when(pl.program_id(0) == 0)
        def _():
            for i in range(lb):
                wide[:, i * width : (i + 1) * width] = x_ref[i]

        res = jnp.dot(w_ref[...], wide[...], preferred_element_type=F32)
        for i in range(lb):
            part = res[:, i * width : (i + 1) * width]
            first_ref[i] = part
            act, _ = gates(g_ref[i].astype(F32))
            turn[pl.ds(i, tj, stride=lb), :] = part * act
        hid_ref[...] = turn[...].reshape(tj, lb, width).astype(BF)

    return pl.pallas_call(
        body,
        grid=(block // tj,),
        in_specs=[
            pl.BlockSpec((lb, block, width), lambda j: (0, 0, 0)),
            pl.BlockSpec((lb, tj, width), lambda j: (0, j, 0)),
            pl.BlockSpec((tj, block), lambda j: (j, 0)),
        ],
        out_specs=[
            pl.BlockSpec((tj, lb, width), lambda j: (j, 0, 0)),
            pl.BlockSpec((lb, tj, width), lambda j: (0, j, 0)),
        ],
        out_shape=[
            jax.ShapeDtypeStruct((block, lb, width), BF),
            jax.ShapeDtypeStruct((lb, block, width), F32),
        ],
        scratch_shapes=[
            pltpu.VMEM((block, lb * width), BF),
            pltpu.VMEM((tj * lb, width), F32),
        ],
        name="front",
    )(x, g, w_first)


def columns(ref, j, rows):
    return ref[:, j].astype(F32).reshape(rows, LANES).astype(BF)


def middle_back(cot_t, w_second_t, tj):
    seq, jp, lb, width = cot_t.shape
    nb = seq * lb

    def body(cot_ref, w_ref, out_ref):
        w = w_ref[...]
        for j in range(0, tj, 2):
            pair = jnp.concatenate([columns(cot_ref, j, nb), columns(cot_ref, j + 1, nb)], axis=1)
            res = jnp.dot(w, pair, preferred_element_type=F32)
            for k in range(2):
                part = res[:, k * width : (k + 1) * width]
                out_ref[:, j + k] = part.reshape(seq, lb, width).astype(BF)

    block = pl.BlockSpec((seq, tj, lb, width), lambda j: (0, j, 0, 0))
    return pl.pallas_call(
        body,
        grid=(jp // tj,),
        in_specs=[block, pl.BlockSpec((nb, nb), lambda j: (0, 0))],
        out_specs=block,
        out_shape=jax.ShapeDtypeStruct(cot_t.shape, BF),
        name="middle_back",
    )(cot_t, w_second_t)


def middle_forward(hid_t, cot_t, w_second, tj):
    seq, jp, lb, width = cot_t.shape
    nb = seq * lb
    steps = jp // tj

    def body(hid_ref, cot_ref, w_ref, out_ref, second_ref, acc):
        step = pl.program_id(0)
        w = w_ref[...]
        total = jnp.zeros((nb, nb), F32)
        for j in range(0, tj, 2):
            pair = jnp.concatenate([columns(hid_ref, j, nb), columns(hid_ref, j + 1, nb)], axis=1)
            res = jnp.dot(w, pair, preferred_element_type=F32)
            for k in range(2):
                part = res[:, k * width : (k + 1) * width]
                out_ref[:, j + k] = part.reshape(seq, lb, width).astype(BF)
            cots = jnp.concatenate([columns(cot_ref, j, nb), columns(cot_ref, j + 1, nb)], axis=1)
            total += lax.dot_general(
                cots, pair, (((1,), (1,)), ((), ())), preferred_element_type=F32
            )

        @pl.when(step == 0)
        def _():
            acc[...] = total

        @pl.when(step > 0)
        def _():
            acc[...] += total

        @pl.when(step == steps - 1)
        def _():
            for k in range(nb // LANES):
                part = acc[:, k * LANES : (k + 1) * LANES]
                second_ref[:, k] = part.reshape(nb // 8, 8, LANES).astype(BF)

    block = pl.BlockSpec((seq, tj, lb, width), lambda j: (0, j, 0, 0))
    tiles = (nb // 8, nb // LANES, 8, LANES)
    return pl.pallas_call(
        body,
        grid=(steps,),
        in_specs=[block, block, pl.BlockSpec((nb, nb), lambda j: (0, 0))],
        out_specs=[block, pl.BlockSpec(tiles, lambda j: (0, 0, 0, 0))],
        out_shape=[
            jax.ShapeDtypeStruct(cot_t.shape, BF),
            jax.ShapeDtypeStruct(tiles, BF),
        ],
        scratch_shapes=[pltpu.VMEM((nb, nb), F32)],
        name="middle_forward",
    )(hid_t, cot_t, w_second)


def back(core, gh, first, x, g, w_first, tj):
    lb, block, width = x.shape
    steps = block // tj
    half = steps // 2
    tiles = block // LANES

    def body(core_ref, gh_ref, first_ref, x_ref, g_ref, w_ref, gate_ref, tok_ref, term_ref,
             wide, gfa, turn):
        step = pl.program_id(0)
        jb = (step + (1 - core_ref[0]) * half) % steps

        @pl.when(step == 0)
        def _():
            for i in range(lb):
                wide[:, i * width : (i + 1) * width] = x_ref[i]

        turn[...] = gh_ref[...].astype(F32).reshape(tj * lb, width)
        at = pl.multiple_of(jb * tj, tj)
        for i in range(lb):
            gh_i = turn[pl.ds(i, tj, stride=lb), :]
            act, slope = gates(g_ref[i].astype(F32))
            gfa[pl.ds(at, tj), i * width : (i + 1) * width] = (gh_i * act).astype(BF)
            gate_ref[i] = (gh_i * first_ref[i] * slope).astype(BF)
        term = lax.dot_general(
            gfa[pl.ds(at, tj), :], wide[...], (((1,), (1,)), ((), ())), preferred_element_type=F32
        )
        for k in range(tiles):
            part = term[:, k * LANES : (k + 1) * LANES]
            term_ref[:, k] = part.reshape(tj // 8, 8, LANES).astype(BF)

        @pl.when(step == steps - 1)
        def _():
            for i in range(0, lb, 2):
                res = lax.dot_general(
                    w_ref[...], gfa[:, i * width : (i + 2) * width],
                    (((0,), (0,)), ((), ())), preferred_element_type=F32,
                )
                tok_ref[i] = res[:, :width].astype(BF)
                tok_ref[i + 1] = res[:, width:].astype(BF)

    def at_block(j, core_ref):
        return (j + (1 - core_ref[0]) * half) % steps

    grid_spec = pltpu.PrefetchScalarGridSpec(
        num_scalar_prefetch=1,
        grid=(steps,),
        in_specs=[
            pl.BlockSpec((tj, lb, width), lambda j, c: (at_block(j, c), 0, 0)),
            pl.BlockSpec((lb, tj, width), lambda j, c: (0, at_block(j, c), 0)),
            pl.BlockSpec((lb, block, width), lambda j, c: (0, 0, 0)),
            pl.BlockSpec((lb, tj, width), lambda j, c: (0, at_block(j, c), 0)),
            pl.BlockSpec((block, block), lambda j, c: (0, 0)),
        ],
        out_specs=[
            pl.BlockSpec((lb, tj, width), lambda j, c: (0, at_block(j, c), 0)),
            pl.BlockSpec((lb, block, width), lambda j, c: (0, 0, 0)),
            pl.BlockSpec((tj // 8, tiles, 8, LANES), lambda j, c: (j, 0, 0, 0)),
        ],
        scratch_shapes=[
            pltpu.VMEM((block, lb * width), BF),
            pltpu.VMEM((block, lb * width), BF),
            pltpu.VMEM((tj * lb, width), F32),
        ],
    )
    return pl.pallas_call(
        body,
        grid_spec=grid_spec,
        out_shape=[
            jax.ShapeDtypeStruct((lb, block, width), BF),
            jax.ShapeDtypeStruct((lb, block, width), BF),
            jax.ShapeDtypeStruct((block // 8, tiles, 8, LANES), BF),
        ],
        name="back",
    )(core, gh, first, x, g, w_first)


def pair_sum(term, taken, second, chips):
    tiles = term.shape[1]

    def body(own_ref, taken_ref, second_ref, out_ref):
        out_ref[:, :tiles] = (own_ref[...].astype(F32) + taken_ref[...].astype(F32)).astype(BF)
        out_ref[:, tiles] = second_ref[...]

    step = chips // 4
    return pl.pallas_call(
        body,
        grid=(4,),
        in_specs=[
            pl.BlockSpec((step, tiles, 8, LANES), lambda p: (p + 4, 0, 0, 0)),
            pl.BlockSpec((step, tiles, 8, LANES), lambda p: (p, 0, 0, 0)),
            pl.BlockSpec((step, 8, LANES), lambda p: (p, 0, 0)),
        ],
        out_specs=pl.BlockSpec((step, tiles + 1, 8, LANES), lambda p: (p, 0, 0, 0)),
        out_shape=jax.ShapeDtypeStruct((chips, tiles + 1, 8, LANES), BF),
        name="pair_sum",
    )(term, taken, second)


def chip_sum(parts):
    def body(in_ref, out_ref):
        total = jnp.sum(in_ref[...].astype(F32), axis=0).astype(BF)
        out_ref[...] = jnp.broadcast_to(total[None], out_ref.shape)

    return pl.pallas_call(
        body, out_shape=jax.ShapeDtypeStruct(parts.shape, BF), name="chip_sum"
    )(parts)


def unpack(core, mine, other, block, nb, scale_first, scale_second):
    chips, tiles = mine.shape[0], mine.shape[1] - 1
    step = chips // 4
    lane_tiles = nb // LANES

    def body(core_ref, mine_ref, other_ref, first_ref, second_ref):
        use_mine = core_ref[0] == pl.program_id(0)

        @pl.when(use_mine)
        def _():
            for k in range(tiles):
                part = mine_ref[:, k].astype(F32) * scale_first
                first_ref[:, k * LANES : (k + 1) * LANES] = part.reshape(step * 8, LANES)

        @pl.when(jnp.logical_not(use_mine))
        def _():
            for k in range(tiles):
                part = other_ref[:, k].astype(F32) * scale_first
                first_ref[:, k * LANES : (k + 1) * LANES] = part.reshape(step * 8, LANES)

        both = mine_ref[:, tiles].astype(F32) + other_ref[:, tiles].astype(F32)
        both = (both * scale_second).reshape(step // lane_tiles, lane_tiles, 8, LANES)
        for k in range(lane_tiles):
            second_ref[:, k * LANES : (k + 1) * LANES] = both[:, k].reshape(-1, LANES)

    spec = pl.BlockSpec((step, tiles + 1, 8, LANES), lambda h, p, c: (p, 0, 0, 0))
    grid_spec = pltpu.PrefetchScalarGridSpec(
        num_scalar_prefetch=1,
        grid=(2, 4),
        in_specs=[spec, spec],
        out_specs=[
            pl.BlockSpec((step * 8, block), lambda h, p, c: (h * 4 + p, 0)),
            pl.BlockSpec((step // lane_tiles * 8, nb), lambda h, p, c: (p, 0)),
        ],
    )
    return pl.pallas_call(
        body,
        grid_spec=grid_spec,
        out_shape=[
            jax.ShapeDtypeStruct((block, block), F32),
            jax.ShapeDtypeStruct((nb, nb), F32),
        ],
        name="unpack",
    )(core, mine, other)


def local(tokens, gate, cotangent, w_first, w_second):
    seq_count = lax.axis_size("seq")
    chan_count = lax.axis_size("ch")
    width = tokens.shape[1]
    block = w_first.shape[0]
    lb = tokens.shape[0] // block
    nb = lb * seq_count
    jp = block // seq_count
    rows = lb * block
    chips = seq_count * chan_count // 2
    same_core = [[2 * k + core for k in range(chips)] for core in range(2)]
    pairs = [(i, i ^ 1) for i in range(chan_count)]
    core = (lax.axis_index("ch") % 2).astype(jnp.int32).reshape(1)

    def exchange(x):
        return lax.all_to_all(x, "seq", split_axis=0, concat_axis=0, tiled=True)

    def chip_exchange(x):
        return lax.all_to_all(
            x, ("seq", "ch"), 0, 0, tiled=True, axis_index_groups=same_core
        )

    x = tokens.reshape(lb, block, width)
    g = gate.reshape(lb, block, width)
    cot = cotangent.reshape(lb, seq_count, jp, width).transpose(1, 2, 0, 3)
    cot_t = exchange(cot)
    hidden, first = front(x, g, w_first, 128)
    hid_t = exchange(hidden.reshape(seq_count, jp, lb, width))
    gh_t = middle_back(cot_t, w_second.T, 8)
    gh_t, hid_t = lax.optimization_barrier((gh_t, hid_t))
    gh_r = exchange(gh_t).reshape(block, lb, width)
    mixed_t, second_term = middle_forward(hid_t, cot_t, w_second, 8)
    mixed_t, gh_r = lax.optimization_barrier((mixed_t, gh_r))
    mixed_r = exchange(mixed_t).reshape(block, lb, width)
    grad_gate, grad_tokens, term = back(core, gh_r, first, x, g, w_first, 128)
    taken = lax.ppermute(term[:chips], "ch", pairs)
    part = pair_sum(term, taken, second_term.reshape(chips, 8, LANES), chips)
    part, mixed_r = lax.optimization_barrier((part, mixed_r))
    part = chip_exchange(part)
    mixed = mixed_r.transpose(1, 0, 2).reshape(rows, width)
    mine = chip_exchange(chip_sum(part))
    other = lax.ppermute(mine, "ch", pairs)
    total_width = width * chan_count
    grad_first, grad_second = unpack(
        core, mine, other, block, nb,
        (nb * total_width) ** -0.5, (block * total_width) ** -0.5,
    )
    return mixed, grad_tokens.reshape(rows, width), grad_gate.reshape(rows, width), grad_first, grad_second


def solution(mesh):
    return jax.shard_map(
        local,
        mesh=mesh,
        in_specs=(P("seq", "ch"), P("seq", "ch"), P("seq", "ch"), P(), P()),
        out_specs=(P("seq", "ch"), P("seq", "ch"), P("seq", "ch"), P(), P()),
        check_vma=False,
    )
```

```python
import jax
import jax.numpy as jnp
from jax import lax
from jax.experimental import pallas as pl
from jax.experimental.pallas import tpu as pltpu
from jax.sharding import PartitionSpec as P

BF = jnp.bfloat16
F32 = jnp.float32
LANES = 128


def gates(g):
    sig = jax.nn.sigmoid(g)
    return g * sig, sig * (1.0 + g * (1.0 - sig))


def front(x, g, w_first, tj):
    lb, block, width = x.shape

    def body(x_ref, g_ref, w_ref, hid_ref, first_ref, wide, turn):
        @pl.when(pl.program_id(0) == 0)
        def _():
            for i in range(lb):
                wide[:, i * width : (i + 1) * width] = x_ref[i]

        res = jnp.dot(w_ref[...], wide[...], preferred_element_type=F32)
        for i in range(lb):
            part = res[:, i * width : (i + 1) * width]
            first_ref[i] = part
            act, _ = gates(g_ref[i].astype(F32))
            turn[pl.ds(i, tj, stride=lb), :] = part * act
        hid_ref[...] = turn[...].reshape(tj, lb, width).astype(BF)

    return pl.pallas_call(
        body,
        grid=(block // tj,),
        in_specs=[
            pl.BlockSpec((lb, block, width), lambda j: (0, 0, 0)),
            pl.BlockSpec((lb, tj, width), lambda j: (0, j, 0)),
            pl.BlockSpec((tj, block), lambda j: (j, 0)),
        ],
        out_specs=[
            pl.BlockSpec((tj, lb, width), lambda j: (j, 0, 0)),
            pl.BlockSpec((lb, tj, width), lambda j: (0, j, 0)),
        ],
        out_shape=[
            jax.ShapeDtypeStruct((block, lb, width), BF),
            jax.ShapeDtypeStruct((lb, block, width), F32),
        ],
        scratch_shapes=[
            pltpu.VMEM((block, lb * width), BF),
            pltpu.VMEM((tj * lb, width), F32),
        ],
        name="front",
    )(x, g, w_first)


def columns(ref, j, rows):
    return ref[:, j].astype(F32).reshape(rows, LANES).astype(BF)


def middle(x_t, w, tj):
    seq, jp, lb, width = x_t.shape
    nb = seq * lb

    def body(x_ref, w_ref, out_ref):
        for j in range(0, tj, 2):
            pair = jnp.concatenate([columns(x_ref, j, nb), columns(x_ref, j + 1, nb)], axis=1)
            res = jnp.dot(w_ref[...], pair, preferred_element_type=F32)
            for k in range(2):
                part = res[:, k * width : (k + 1) * width]
                out_ref[:, j + k] = part.reshape(seq, lb, width).astype(BF)

    block = pl.BlockSpec((seq, tj, lb, width), lambda j: (0, j, 0, 0))
    return pl.pallas_call(
        body,
        grid=(jp // tj,),
        in_specs=[block, pl.BlockSpec((nb, nb), lambda j: (0, 0))],
        out_specs=block,
        out_shape=jax.ShapeDtypeStruct(x_t.shape, BF),
    )(x_t, w)


def sums(hid_t, cot_t, parts, tj):
    seq, jp, lb, width = cot_t.shape
    nb = seq * lb
    steps = jp // tj
    plane, tiles = parts[0].shape[:2]
    lane_tiles = nb // LANES
    extra = nb // 8 * lane_tiles // plane

    def body(hid_ref, cot_ref, *refs):
        part_refs, out_ref, acc = refs[:-2], refs[-2], refs[-1]
        step = pl.program_id(0)
        total = jnp.zeros((nb, nb), F32)
        for j in range(0, tj, 2):
            hids = jnp.concatenate([columns(hid_ref, j, nb), columns(hid_ref, j + 1, nb)], axis=1)
            cots = jnp.concatenate([columns(cot_ref, j, nb), columns(cot_ref, j + 1, nb)], axis=1)
            total += lax.dot_general(
                cots, hids, (((1,), (1,)), ((), ())), preferred_element_type=F32
            )

        @pl.when(step == 0)
        def _():
            acc[...] = total
            main = part_refs[0][...].astype(F32)
            for ref in part_refs[1:]:
                main += ref[...].astype(F32)
            out_ref[:, :tiles] = main.astype(BF)

        @pl.when(step > 0)
        def _():
            acc[...] += total

        @pl.when(step == steps - 1)
        def _():
            for p in range(plane * extra):
                row, lane = divmod(p, lane_tiles)
                out_ref[p // extra, tiles + p % extra] = acc[
                    row * 8 : row * 8 + 8, lane * LANES : (lane + 1) * LANES
                ].astype(BF)

    block = pl.BlockSpec((seq, tj, lb, width), lambda j: (0, j, 0, 0))
    whole = pl.BlockSpec(parts[0].shape, lambda j: (0, 0, 0, 0))
    shape = (plane, tiles + extra, 8, LANES)
    return pl.pallas_call(
        body,
        grid=(steps,),
        in_specs=[block, block] + [whole] * len(parts),
        out_specs=pl.BlockSpec(shape, lambda j: (0, 0, 0, 0)),
        out_shape=jax.ShapeDtypeStruct(shape, BF),
        scratch_shapes=[pltpu.VMEM((nb, nb), F32)],
        name="sums",
    )(hid_t, cot_t, *parts)


def pack(x, tj):
    lb, block, width = x.shape

    def body(x_ref, out_ref, turn):
        for i in range(lb):
            turn[pl.ds(i, tj, stride=lb), :] = x_ref[i].astype(F32)
        out_ref[...] = turn[...].reshape(tj, lb, width).astype(BF)

    return pl.pallas_call(
        body,
        grid=(block // tj,),
        in_specs=[pl.BlockSpec((lb, tj, width), lambda j: (0, j, 0))],
        out_specs=pl.BlockSpec((tj, lb, width), lambda j: (j, 0, 0)),
        out_shape=jax.ShapeDtypeStruct((block, lb, width), BF),
        scratch_shapes=[pltpu.VMEM((tj * lb, width), F32)],
        name="pack",
    )(x)


def unfold(x, tj):
    block, lb, width = x.shape

    def body(x_ref, out_ref, turn):
        turn[...] = x_ref[...].astype(F32).reshape(tj * lb, width)
        for i in range(lb):
            out_ref[i] = turn[pl.ds(i, tj, stride=lb), :].astype(BF)

    return pl.pallas_call(
        body,
        grid=(block // tj,),
        in_specs=[pl.BlockSpec((tj, lb, width), lambda j: (j, 0, 0))],
        out_specs=pl.BlockSpec((lb, tj, width), lambda j: (0, j, 0)),
        out_shape=jax.ShapeDtypeStruct((lb, block, width), BF),
        scratch_shapes=[pltpu.VMEM((tj * lb, width), F32)],
        name="unfold",
    )(x)


def back(where, gh, first, x, g, tj):
    lb, block, width = x.shape
    steps = block // tj
    half = steps // 2
    tiles = block // LANES

    def body(where_ref, gh_ref, first_ref, x_ref, g_ref, gate_ref, gfa_ref, give_ref, own_ref,
             wide, turn):
        step = pl.program_id(0)

        @pl.when(step == 0)
        def _():
            for i in range(lb):
                wide[:, i * width : (i + 1) * width] = x_ref[i]

        turn[...] = gh_ref[...].astype(F32).reshape(tj * lb, width)
        for i in range(lb):
            gh_i = turn[pl.ds(i, tj, stride=lb), :]
            act, slope = gates(g_ref[i].astype(F32))
            gfa_ref[:, i * width : (i + 1) * width] = (gh_i * act).astype(BF)
            gate_ref[i] = (gh_i * first_ref[i] * slope).astype(BF)
        term = lax.dot_general(
            gfa_ref[...], wide[...], (((1,), (1,)), ((), ())), preferred_element_type=F32
        )

        def store(ref):
            for k in range(tiles):
                part = term[:, k * LANES : (k + 1) * LANES]
                ref[:, k] = part.reshape(tj // 8, 8, LANES).astype(BF)

        @pl.when(step < half)
        def _():
            store(give_ref)

        @pl.when(step >= half)
        def _():
            store(own_ref)

    def at(j, where_ref):
        return (j + (1 - where_ref[0]) * half) % steps

    piece = (tj // 8, tiles, 8, LANES)
    grid_spec = pltpu.PrefetchScalarGridSpec(
        num_scalar_prefetch=1,
        grid=(steps,),
        in_specs=[
            pl.BlockSpec((tj, lb, width), lambda j, c: (at(j, c), 0, 0)),
            pl.BlockSpec((lb, tj, width), lambda j, c: (0, at(j, c), 0)),
            pl.BlockSpec((lb, block, width), lambda j, c: (0, 0, 0)),
            pl.BlockSpec((lb, tj, width), lambda j, c: (0, at(j, c), 0)),
        ],
        out_specs=[
            pl.BlockSpec((lb, tj, width), lambda j, c: (0, at(j, c), 0)),
            pl.BlockSpec((tj, lb * width), lambda j, c: (at(j, c), 0)),
            pl.BlockSpec(piece, lambda j, c: (jnp.minimum(j, half - 1), 0, 0, 0)),
            pl.BlockSpec(piece, lambda j, c: (jnp.maximum(j - half, 0), 0, 0, 0)),
        ],
        scratch_shapes=[
            pltpu.VMEM((block, lb * width), BF),
            pltpu.VMEM((tj * lb, width), F32),
        ],
    )
    half_shape = (block // 16, tiles, 8, LANES)
    return pl.pallas_call(
        body,
        grid_spec=grid_spec,
        out_shape=[
            jax.ShapeDtypeStruct((lb, block, width), BF),
            jax.ShapeDtypeStruct((block, lb * width), BF),
            jax.ShapeDtypeStruct(half_shape, BF),
            jax.ShapeDtypeStruct(half_shape, BF),
        ],
        name="back",
    )(where, gh, first, x, g)


def back_tokens(gfa, w_first, width):
    block, wide = gfa.shape
    lb = wide // width

    def body(gfa_ref, w_ref, out_ref):
        res = lax.dot_general(
            w_ref[...], gfa_ref[...], (((0,), (0,)), ((), ())), preferred_element_type=F32
        )
        out_ref[0] = res[:, :width].astype(BF)
        out_ref[1] = res[:, width:].astype(BF)

    return pl.pallas_call(
        body,
        grid=(lb // 2,),
        in_specs=[
            pl.BlockSpec((block, 2 * width), lambda i: (0, i)),
            pl.BlockSpec((block, block), lambda i: (0, 0)),
        ],
        out_specs=pl.BlockSpec((2, block, width), lambda i: (i, 0, 0)),
        out_shape=jax.ShapeDtypeStruct((lb, block, width), BF),
        name="back_tokens",
    )(gfa, w_first)


def pair_sum(where, own, taken, ring):
    chips, tiles = own.shape[:2]
    step = chips // ring

    def body(where_ref, own_ref, taken_ref, *outs):
        for d in range(ring):
            at = pl.ds(((where_ref[1] + d) % ring) * step, step)
            outs[d][...] = (own_ref[at].astype(F32) + taken_ref[at].astype(F32)).astype(BF)

    vm = pl.BlockSpec(memory_space=pltpu.VMEM)
    return pl.pallas_call(
        body,
        in_specs=[pl.BlockSpec(memory_space=pltpu.SMEM), vm, vm],
        out_specs=[vm] * ring,
        out_shape=[jax.ShapeDtypeStruct((step, tiles, 8, LANES), BF)] * ring,
        name="pair_sum",
    )(where, own, taken)


def plane_sum(parts):
    def body(in_ref, out_ref):
        out_ref[0] = jnp.sum(in_ref[...].astype(F32), axis=0).astype(BF)

    return pl.pallas_call(
        body, out_shape=jax.ShapeDtypeStruct((1,) + parts.shape[1:], BF), name="plane_sum"
    )(parts)


def z_sum(got, tiles):
    ring = len(got)
    extra = got[0].shape[1] - tiles

    def body(*refs):
        out_ref = refs[-1]
        total = jnp.zeros((extra, 8, LANES), F32)
        for d in range(ring):
            out_ref[0, d * tiles : (d + 1) * tiles] = refs[d][0, :tiles]
            total += refs[d][0, tiles:].astype(F32)
        out_ref[0, ring * tiles :] = total.astype(BF)

    return pl.pallas_call(
        body,
        out_shape=jax.ShapeDtypeStruct((1, ring * tiles + extra, 8, LANES), BF),
        name="z_sum",
    )(*got)


def unpack(where, mine, other, block, nb, tiles, scale_first, scale_second):
    ring = len(mine)
    lane_tiles = nb // LANES
    extra = mine[0].shape[1] - ring * tiles
    plane = ring * ring

    def body(where_ref, *refs):
        mine_refs, other_refs = refs[:ring], refs[ring : 2 * ring]
        first_ref, second_ref, both = refs[2 * ring :]
        core, z, y, x = (where_ref[k] for k in range(4))
        for dy in range(ring):
            for dx in range(ring):
                spot = ((y - dy + ring) % ring) * ring + (x - dx + ring) % ring
                for dz in range(ring):
                    chip = ((z - dz + ring) % ring) * plane + spot
                    for ref, c in ((mine_refs[dy], core), (other_refs[dy], 1 - core)):
                        row = pl.multiple_of(c * (block // 2) + chip * 8, 8)
                        for k in range(tiles):
                            first_ref[pl.ds(row, 8), k * LANES : (k + 1) * LANES] = (
                                ref[dx, dz * tiles + k].astype(F32) * scale_first
                            )
                total = mine_refs[dy][dx, ring * tiles :].astype(F32)
                total += other_refs[dy][dx, ring * tiles :].astype(F32)
                both[pl.ds(spot * extra, extra)] = total * scale_second
        for p in range(plane * extra):
            row, lane = divmod(p, lane_tiles)
            second_ref[row * 8 : row * 8 + 8, lane * LANES : (lane + 1) * LANES] = both[p]

    vm = pl.BlockSpec(memory_space=pltpu.VMEM)
    return pl.pallas_call(
        body,
        in_specs=[pl.BlockSpec(memory_space=pltpu.SMEM)] + [vm] * (2 * ring),
        out_specs=[vm, vm],
        out_shape=[
            jax.ShapeDtypeStruct((block, block), F32),
            jax.ShapeDtypeStruct((nb, nb), F32),
        ],
        scratch_shapes=[pltpu.VMEM((plane * extra, 8, LANES), F32)],
        name="unpack",
    )(where, *mine, *other)


def local(tokens, gate, cotangent, w_first, w_second):
    seq_count = lax.axis_size("seq")
    chan_count = lax.axis_size("ch")
    width = tokens.shape[1]
    block = w_first.shape[0]
    lb = tokens.shape[0] // block
    nb = lb * seq_count
    jp = block // seq_count
    rows = lb * block
    ring = 4
    plane = ring * ring
    seq_at, ch_at = lax.axis_index("seq"), lax.axis_index("ch")
    where = jnp.stack([
        ch_at % 2, seq_at // plane * 2 + ch_at // 2, seq_at // ring % ring, seq_at % ring
    ]).astype(jnp.int32)

    def device(core, z, y, x):
        return ((z // 2 * plane + y * ring + x) * 2 + z % 2) * 2 + core

    every = [(c, z, y, x) for c in range(2) for z in range(ring) for y in range(ring)
             for x in range(ring)]

    def shift(value, axis, d):
        pairs = []
        for at in every:
            to = list(at)
            to[axis] = (to[axis] + d) % (ring if axis else 2)
            pairs.append((device(*at), device(*to)))
        return lax.ppermute(value, ("seq", "ch"), pairs)

    planes = [[device(c, z, y, x) for y in range(ring) for x in range(ring)]
              for c in range(2) for z in range(ring)]

    def exchange(x):
        return lax.all_to_all(x, "seq", split_axis=0, concat_axis=0, tiled=True)

    def ring_gather(value, axis):
        return [value] + [shift(value, axis, d) for d in range(1, ring)]

    x = tokens.reshape(lb, block, width)
    g = gate.reshape(lb, block, width)
    cot = pack(cotangent.reshape(lb, block, width), 256)
    cot_t = exchange(cot.reshape(seq_count, jp, lb, width))
    hidden, first = front(x, g, w_first, 256)
    gh_t = middle(cot_t, w_second.T, 8)
    gh_r = exchange(gh_t).reshape(block, lb, width)
    hidden, gh_r = lax.optimization_barrier((hidden, gh_r))
    hid_t = exchange(hidden.reshape(seq_count, jp, lb, width))
    grad_gate, gfa, give, own = back(where, gh_r, first, x, g, 256)
    tiles = own.shape[1]
    taken = shift(give, 0, 1)
    parts = pair_sum(where, own, taken, ring)
    parts = [parts[0]] + [shift(parts[d], 1, d) for d in range(1, ring)]
    part = sums(hid_t, cot_t, parts, 8)
    part = lax.all_to_all(
        part, ("seq", "ch"), 0, 0, tiled=True, axis_index_groups=planes
    )
    mixed_t = middle(hid_t, w_second, 8)
    grad_tokens = back_tokens(gfa, w_first, width)
    mixed_t, part = lax.optimization_barrier((mixed_t, part))
    mixed_r = exchange(mixed_t).reshape(block, lb, width)
    mine = z_sum(ring_gather(plane_sum(part), 1), tiles)
    mine = jnp.concatenate(ring_gather(mine, 3))
    mine = ring_gather(mine, 2)
    other = [shift(value, 0, 1) for value in mine]
    total_width = width * chan_count
    grad_first, grad_second = unpack(
        where, mine, other, block, nb, tiles,
        (nb * total_width) ** -0.5, (block * total_width) ** -0.5,
    )
    mixed = unfold(mixed_r, 256).reshape(rows, width)
    return mixed, grad_tokens.reshape(rows, width), grad_gate.reshape(rows, width), grad_first, grad_second


def solution(mesh):
    return jax.shard_map(
        local,
        mesh=mesh,
        in_specs=(P("seq", "ch"), P("seq", "ch"), P("seq", "ch"), P(), P()),
        out_specs=(P("seq", "ch"), P("seq", "ch"), P("seq", "ch"), P(), P()),
        check_vma=False,
    )
```

```python
import jax
import jax.numpy as jnp
from jax import lax
from jax.experimental import pallas as pl
from jax.experimental.pallas import tpu as pltpu
from jax.sharding import PartitionSpec as P

BF = jnp.bfloat16
F32 = jnp.float32
LANES = 128
MIB = 1 << 20


def gates(g):
    sig = jax.nn.sigmoid(g)
    return g * sig, sig * (1.0 + g * (1.0 - sig))


def in_vmem(x):
    return pltpu.with_memory_space_constraint(x, pltpu.VMEM)


def in_hbm(x):
    return pltpu.with_memory_space_constraint(x, pltpu.HBM)


WHOLE = pl.BlockSpec(memory_space=pltpu.VMEM)


def front(x, g, w_first, seq, tj):
    lb, block, width = x.shape
    jp = block // seq

    def body(x_ref, g_ref, w_ref, hid_ref, first_ref, wide, turn):
        @pl.when(pl.program_id(0) == 0)
        def _():
            for i in range(lb):
                wide[:, i * width : (i + 1) * width] = x_ref[i]

        res = jnp.dot(w_ref[...], wide[...], preferred_element_type=F32)
        for i in range(lb):
            part = res[:, i * width : (i + 1) * width]
            first_ref[i] = part
            act, _ = gates(g_ref[i].astype(F32))
            turn[pl.ds(i, tj, stride=lb), :] = part * act
        hid_ref[...] = turn[...].reshape(tj // jp, jp, lb, width).astype(BF)

    return pl.pallas_call(
        body,
        grid=(block // tj,),
        in_specs=[
            pl.BlockSpec((lb, block, width), lambda j: (0, 0, 0)),
            pl.BlockSpec((lb, tj, width), lambda j: (0, j, 0)),
            pl.BlockSpec((tj, block), lambda j: (j, 0)),
        ],
        out_specs=[
            pl.BlockSpec((tj // jp, jp, lb, width), lambda j: (j, 1, 0, 0)),
            pl.BlockSpec((lb, tj, width), lambda j: (0, j, 0)),
        ],
        out_shape=[
            pltpu.HBM((seq, 2 * jp, lb, width), BF),
            pltpu.HBM((lb, block, width), F32),
        ],
        scratch_shapes=[
            pltpu.VMEM((block, lb * width), BF),
            pltpu.VMEM((tj * lb, width), F32),
        ],
        name="front",
        compiler_params=pltpu.CompilerParams(vmem_limit_bytes=28 * MIB),
    )(in_hbm(x), in_hbm(g), in_hbm(w_first))


def columns(ref, j, rows):
    return ref[:, j].astype(F32).reshape(rows, LANES).astype(BF)


def pair(ref, j, rows):
    return jnp.concatenate([columns(ref, j, rows), columns(ref, j + 1, rows)], axis=1)


def middle(x_t, w, tj, first_row, into=None):
    seq, lb, width = x_t.shape[0], x_t.shape[2], x_t.shape[3]
    nb = seq * lb
    jp = x_t.shape[1] - first_row
    kept = into is not None

    def body(x_ref, w_ref, *refs):
        out_ref = refs[-1]
        base = pl.program_id(0) * tj if kept else 0
        for j in range(0, tj, 2):
            res = jnp.dot(w_ref[...], pair(x_ref, base + j, nb), preferred_element_type=F32)
            for k in range(2):
                part = res[:, k * width : (k + 1) * width]
                out_ref[:, j + k] = part.reshape(seq, lb, width).astype(BF)

    def block(row):
        return pl.BlockSpec((seq, tj, lb, width), lambda j: (0, row // tj + j, 0, 0))

    return pl.pallas_call(
        body,
        grid=(jp // tj,),
        in_specs=[WHOLE if kept else block(first_row), pl.BlockSpec((nb, nb), lambda j: (0, 0))]
        + [pl.BlockSpec(memory_space=pl.ANY)] * kept,
        out_specs=block(0),
        out_shape=pltpu.HBM(into.shape if kept else (seq, jp, lb, width), BF),
        input_output_aliases={2: 0} if kept else {},
        name="middle_back" if kept else "middle_forward",
        compiler_params=pltpu.CompilerParams(vmem_limit_bytes=16 * MIB),
    )(*([in_vmem(x_t), w, in_hbm(into)] if kept else [in_hbm(x_t), w]))


def second(cot_t, hid_t, first_row, tj):
    seq, jp, lb, width = cot_t.shape
    nb = seq * lb
    steps = jp // tj
    tiles = (nb // 8, nb // LANES, 8, LANES)

    def body(cot_ref, hid_ref, out_ref, acc):
        step = pl.program_id(0)
        total = jnp.zeros((nb, nb), F32)
        for j in range(0, tj, 2):
            total += lax.dot_general(
                pair(cot_ref, step * tj + j, nb), pair(hid_ref, j, nb),
                (((1,), (1,)), ((), ())), preferred_element_type=F32,
            )

        @pl.when(step == 0)
        def _():
            acc[...] = total

        @pl.when(step > 0)
        def _():
            acc[...] += total

        @pl.when(step == steps - 1)
        def _():
            for k in range(nb // LANES):
                part = acc[:, k * LANES : (k + 1) * LANES]
                out_ref[:, k] = part.reshape(nb // 8, 8, LANES).astype(BF)

    return pl.pallas_call(
        body,
        grid=(steps,),
        in_specs=[
            WHOLE,
            pl.BlockSpec((seq, tj, lb, width), lambda j: (0, first_row // tj + j, 0, 0)),
        ],
        out_specs=WHOLE,
        out_shape=pltpu.VMEM(tiles, BF),
        scratch_shapes=[pltpu.VMEM((nb, nb), F32)],
        name="second",
        compiler_params=pltpu.CompilerParams(vmem_limit_bytes=16 * MIB),
    )(in_vmem(cot_t), in_hbm(hid_t))


def pack(x, tj):
    lb, block, width = x.shape

    def body(x_ref, out_ref, turn):
        for i in range(lb):
            turn[pl.ds(i, tj, stride=lb), :] = x_ref[i].astype(F32)
        out_ref[...] = turn[...].reshape(tj, lb, width).astype(BF)

    return pl.pallas_call(
        body,
        grid=(block // tj,),
        in_specs=[pl.BlockSpec((lb, tj, width), lambda j: (0, j, 0))],
        out_specs=pl.BlockSpec((tj, lb, width), lambda j: (j, 0, 0)),
        out_shape=pltpu.HBM((block, lb, width), BF),
        scratch_shapes=[pltpu.VMEM((tj * lb, width), F32)],
        name="pack",
        compiler_params=pltpu.CompilerParams(vmem_limit_bytes=8 * MIB),
    )(in_hbm(x))


def unfold(x, tj):
    block, lb, width = x.shape

    def body(x_ref, out_ref, turn):
        turn[...] = x_ref[...].astype(F32).reshape(tj * lb, width)
        for i in range(lb):
            out_ref[i] = turn[pl.ds(i, tj, stride=lb), :].astype(BF)

    return pl.pallas_call(
        body,
        grid=(block // tj,),
        in_specs=[pl.BlockSpec((tj, lb, width), lambda j: (j, 0, 0))],
        out_specs=pl.BlockSpec((lb, tj, width), lambda j: (0, j, 0)),
        out_shape=pltpu.HBM((lb, block, width), BF),
        scratch_shapes=[pltpu.VMEM((tj * lb, width), F32)],
        name="unfold",
        compiler_params=pltpu.CompilerParams(vmem_limit_bytes=8 * MIB),
    )(x)


def back(where, gh, first, x, g, tj):
    lb, block, width = x.shape
    steps = block // tj
    half = steps // 2
    tiles = block // LANES
    jp = block // gh.shape[0]

    def body(where_ref, gh_ref, first_ref, x_ref, g_ref, gate_ref, gfa_ref, give_ref, own_ref,
             wide, turn):
        step = pl.program_id(0)

        @pl.when(step == 0)
        def _():
            for i in range(lb):
                wide[:, i * width : (i + 1) * width] = x_ref[i]

        turn[...] = gh_ref[...].astype(F32).reshape(tj * lb, width)
        for i in range(lb):
            gh_i = turn[pl.ds(i, tj, stride=lb), :]
            act, slope = gates(g_ref[i].astype(F32))
            gfa_ref[:, i * width : (i + 1) * width] = (gh_i * act).astype(BF)
            gate_ref[i] = (gh_i * first_ref[i] * slope).astype(BF)
        term = lax.dot_general(
            gfa_ref[...], wide[...], (((1,), (1,)), ((), ())), preferred_element_type=F32
        )

        def store(ref):
            for k in range(tiles):
                part = term[:, k * LANES : (k + 1) * LANES]
                ref[:, k] = part.reshape(tj // 8, 8, LANES).astype(BF)

        @pl.when(step < half)
        def _():
            store(give_ref)

        @pl.when(step >= half)
        def _():
            store(own_ref)

    def at(j, where_ref):
        return (j + (1 - where_ref[0]) * half) % steps

    piece = (tj // 8, tiles, 8, LANES)
    grid_spec = pltpu.PrefetchScalarGridSpec(
        num_scalar_prefetch=1,
        grid=(steps,),
        in_specs=[
            pl.BlockSpec((tj // jp, jp, lb, width), lambda j, c: (at(j, c), 0, 0, 0)),
            pl.BlockSpec((lb, tj, width), lambda j, c: (0, at(j, c), 0)),
            pl.BlockSpec((lb, block, width), lambda j, c: (0, 0, 0)),
            pl.BlockSpec((lb, tj, width), lambda j, c: (0, at(j, c), 0)),
        ],
        out_specs=[
            pl.BlockSpec((lb, tj, width), lambda j, c: (0, at(j, c), 0)),
            pl.BlockSpec((tj, lb * width), lambda j, c: (at(j, c), 0)),
            pl.BlockSpec(piece, lambda j, c: (jnp.minimum(j, half - 1), 0, 0, 0)),
            pl.BlockSpec(piece, lambda j, c: (jnp.maximum(j - half, 0), 0, 0, 0)),
        ],
        scratch_shapes=[
            pltpu.VMEM((block, lb * width), BF),
            pltpu.VMEM((tj * lb, width), F32),
        ],
    )
    half_shape = (block // 16, tiles, 8, LANES)
    return pl.pallas_call(
        body,
        grid_spec=grid_spec,
        out_shape=[
            pltpu.HBM((lb, block, width), BF),
            pltpu.HBM((block, lb * width), BF),
            pltpu.HBM(half_shape, BF),
            pltpu.HBM(half_shape, BF),
        ],
        name="back",
        compiler_params=pltpu.CompilerParams(vmem_limit_bytes=28 * MIB),
    )(where, in_hbm(gh), in_hbm(first), in_hbm(x), in_hbm(g))


def back_tokens(gfa, w_first, width):
    block, wide = gfa.shape
    lb = wide // width

    def body(gfa_ref, w_ref, out_ref):
        res = lax.dot_general(
            w_ref[...], gfa_ref[...], (((0,), (0,)), ((), ())), preferred_element_type=F32
        )
        out_ref[0] = res[:, :width].astype(BF)
        out_ref[1] = res[:, width:].astype(BF)

    return pl.pallas_call(
        body,
        grid=(lb // 2,),
        in_specs=[
            pl.BlockSpec((block, 2 * width), lambda i: (0, i)),
            pl.BlockSpec((block, block), lambda i: (0, 0)),
        ],
        out_specs=pl.BlockSpec((2, block, width), lambda i: (i, 0, 0)),
        out_shape=pltpu.HBM((lb, block, width), BF),
        name="back_tokens",
        compiler_params=pltpu.CompilerParams(vmem_limit_bytes=20 * MIB),
    )(in_hbm(gfa), in_hbm(w_first))


def pair_sum(own, taken, second_term):
    chips, tiles = own.shape[:2]

    def body(own_ref, taken_ref, second_ref, out_ref):
        out_ref[:, :tiles] = (own_ref[...].astype(F32) + taken_ref[...].astype(F32)).astype(BF)
        out_ref[:, tiles] = second_ref[...]

    return pl.pallas_call(
        body,
        in_specs=[WHOLE] * 3,
        out_specs=WHOLE,
        out_shape=pltpu.VMEM((chips, tiles + 1, 8, LANES), BF),
        name="pair_sum",
        compiler_params=pltpu.CompilerParams(vmem_limit_bytes=16 * MIB),
    )(own, in_vmem(taken), in_vmem(second_term))


def chip_sum(parts):
    def body(in_ref, out_ref):
        total = jnp.sum(in_ref[...].astype(F32), axis=0).astype(BF)
        out_ref[...] = jnp.broadcast_to(total[None], out_ref.shape)

    return pl.pallas_call(
        body,
        in_specs=[WHOLE],
        out_specs=WHOLE,
        out_shape=pltpu.VMEM(parts.shape, BF),
        name="chip_sum",
        compiler_params=pltpu.CompilerParams(vmem_limit_bytes=12 * MIB),
    )(in_vmem(parts))


def unpack(where, mine, other, block, nb, scale_first, scale_second):
    chips, tiles = mine.shape[0], mine.shape[1] - 1
    lane_tiles = nb // LANES
    half = chips * 8

    def body(where_ref, mine_ref, other_ref, first_ref, second_ref):
        core = where_ref[0]
        for ref, c in ((mine_ref, core), (other_ref, 1 - core)):
            rows = pl.ds(pl.multiple_of(c * half, half), half)
            for k in range(tiles):
                part = ref[:, k].astype(F32) * scale_first
                first_ref[rows, k * LANES : (k + 1) * LANES] = part.reshape(half, LANES)
        both = mine_ref[:, tiles].astype(F32) + other_ref[:, tiles].astype(F32)
        both = (both * scale_second).reshape(chips // lane_tiles, lane_tiles, 8, LANES)
        for k in range(lane_tiles):
            second_ref[:, k * LANES : (k + 1) * LANES] = both[:, k].reshape(-1, LANES)

    return pl.pallas_call(
        body,
        in_specs=[pl.BlockSpec(memory_space=pltpu.SMEM), WHOLE, WHOLE],
        out_specs=[WHOLE, WHOLE],
        out_shape=[
            jax.ShapeDtypeStruct((block, block), F32),
            jax.ShapeDtypeStruct((nb, nb), F32),
        ],
        name="unpack",
        compiler_params=pltpu.CompilerParams(vmem_limit_bytes=16 * MIB),
    )(where, in_vmem(mine), in_vmem(other))


def local(tokens, gate, cotangent, w_first, w_second):
    seq_count = lax.axis_size("seq")
    chan_count = lax.axis_size("ch")
    width = tokens.shape[1]
    block = w_first.shape[0]
    lb = tokens.shape[0] // block
    nb = lb * seq_count
    jp = block // seq_count
    rows = lb * block
    chips = seq_count * chan_count // 2
    same_core = [[2 * k + core for k in range(chips)] for core in range(2)]
    pairs = [(i, i ^ 1) for i in range(chan_count)]
    where = (lax.axis_index("ch") % 2).astype(jnp.int32).reshape(1)

    def exchange(x):
        return lax.all_to_all(x, "seq", split_axis=0, concat_axis=0, tiled=True)

    def chip_exchange(x):
        return lax.all_to_all(
            x, ("seq", "ch"), 0, 0, tiled=True, axis_index_groups=same_core
        )

    x = tokens.reshape(lb, block, width)
    g = gate.reshape(lb, block, width)
    cot = pack(cotangent.reshape(lb, block, width), 256)
    cot_t = exchange(cot.reshape(seq_count, jp, lb, width))
    both, first = front(x, g, w_first, seq_count, 256)
    both = middle(cot_t, w_second.T, 8, 0, both)
    both = exchange(both)
    mixed_t = middle(both, w_second, 8, jp)
    mixed_r = exchange(mixed_t).reshape(block, lb, width)
    grad_gate, gfa, give, own = back(where, both, first, x, g, 256)
    taken = lax.ppermute(give, "ch", pairs)
    second_term = second(cot_t, both, jp, 8)
    part = pair_sum(own, taken, second_term.reshape(chips, 8, LANES))
    grad_tokens = back_tokens(gfa, w_first, width)
    part, grad_tokens, mixed_r = lax.optimization_barrier((part, grad_tokens, mixed_r))
    part = chip_exchange(part)
    mixed = unfold(mixed_r, 256).reshape(rows, width)
    mine = chip_exchange(chip_sum(part))
    other = lax.ppermute(mine, "ch", pairs)
    total_width = width * chan_count
    grad_first, grad_second = unpack(
        where, mine, other, block, nb,
        (nb * total_width) ** -0.5, (block * total_width) ** -0.5,
    )
    return mixed, grad_tokens.reshape(rows, width), grad_gate.reshape(rows, width), grad_first, grad_second


def solution(mesh):
    return jax.shard_map(
        local,
        mesh=mesh,
        in_specs=(P("seq", "ch"), P("seq", "ch"), P("seq", "ch"), P(), P()),
        out_specs=(P("seq", "ch"), P("seq", "ch"), P("seq", "ch"), P(), P()),
        check_vma=False,
    )
```
